32 devices in a mesh: grp: 2 (over y), seq: 16 (over z, x, core).
Axes of the slice: x: 2, y: 2, z: 4, core: 2. Of those that a mesh axis runs over, the one named last changes fastest.
Arguments:
- queries: bfloat16 [8192, 2048], P(('grp', 'seq')), parts along dimension 0, may hold values from -6 to 6
- keys: bfloat16 [8192, 2048], P(('grp', 'seq')), parts along dimension 0, may hold values from -6 to 6
- values: bfloat16 [8192, 2048], P(('grp', 'seq')), parts along dimension 0, may hold values from -6 to 6
- feature_map: bfloat16 [16, 128, 128], replicated, may hold values from -0.5 to 0.5
- out_grad: bfloat16 [8192, 2048], P(('grp', 'seq')), parts along dimension 0, may hold values from -6 to 6
Outputs:
- attended: bfloat16 [8192, 2048], P(('grp', 'seq')), parts along dimension 0
- query_grad: bfloat16 [8192, 2048], P(('grp', 'seq')), parts along dimension 0
- key_grad: bfloat16 [8192, 2048], P(('grp', 'seq')), parts along dimension 0
- value_grad: bfloat16 [8192, 2048], P(('grp', 'seq')), parts along dimension 0
- feature_grad: float32 [524288], P(('grp', 'seq')), parts along dimension 0
The draws below stay inside these ranges and needn't reach their ends.
There are 2 independent parts, one for each index of `grp`. The reference program is written for one: setup_inputs(seed, part) draws one part's arguments, and reference() takes and returns one part's arrays. A program takes and returns all parts, laid end to end along the dimension named above; an argument that names none is the same for every part. Nothing has to cross between parts.
All inputs are finite; a program needn't handle non-finite values.
Results may differ from the reference program's by a relative error of at most 0.0085.
Values may be sent and summed in bfloat16 or wider, within the bound.
A program may use at most 64 MiB of HBM per device.

```python
import math
import jax
import jax.numpy as jnp
from jax import lax

HEADS = 16
DH = 128
TOK_DEV = 256
TOKENS = 4096


def strengthened(array, key, source, target, shards_of, factor):
    def block_of(axis_at):
        return (jnp.arange(array.shape[axis_at]) // (array.shape[axis_at] // shards_of)).reshape((-1,) + (1,) * (array.ndim - 1 - axis_at))

    near = jax.random.permutation(key, shards_of)[block_of(target)]
    far = (block_of(target) + shards_of // 2) % shards_of
    return jnp.where((block_of(source) == near) | (block_of(source) == far), factor * array, array)


def levels(stream_key, extent, split, least, high):
    gain, own = 1.0, jax.random.fold_in(stream_key, 6)
    for axis_at, blocks in split:
        heights = jnp.exp(jax.random.uniform(jax.random.fold_in(own, axis_at), (blocks,), jnp.float32, least / len(split), high / len(split)))
        gain = gain * jnp.repeat(heights, extent[axis_at] // blocks).reshape([-1 if axis == axis_at else 1 for axis in range(len(extent))])
    return gain


def normal_values(stream_key, dims, width, reach, pieces=(), dtype=jnp.bfloat16):
    gain = levels(stream_key, dims, pieces, -0.22, 0.18) if pieces else 1.0
    array = jax.random.normal(stream_key, dims, jnp.float32) * width * gain
    return jnp.minimum(jnp.maximum(array, -reach), reach).astype(dtype)


def gaussian_with(key, shape, spread, most, shards, heavy, held_as=jnp.bfloat16):
    entries = spread * jax.random.normal(key, shape, jnp.float32)
    if shards:
        entries = entries * levels(key, shape, shards, -0.22, 0.18)
    return jnp.clip(strengthened(entries, jax.random.fold_in(key, 3), *heavy), -most, most).astype(held_as)


def setup_inputs(seed: int = 0, part: int = 0) -> dict:
    streams_of = jax.random.split(jax.random.key(seed), 6)
    own_keys = jax.random.split(jax.random.fold_in(streams_of[5], part), 6)
    return {
        "queries": gaussian_with(own_keys[0], (TOKENS, HEADS * DH), 1.0, 6.0, ((0, 16),), (0, 1, 16, 2.0)),
        "keys": normal_values(own_keys[1], (TOKENS, HEADS * DH), 1.0, 6.0, ((0, 16),)),
        "values": normal_values(own_keys[2], (TOKENS, HEADS * DH), 1.0, 6.0, ((0, 16),)),
        "feature_map": normal_values(streams_of[3], (HEADS, DH, DH), DH ** -0.5, 0.5),
        "out_grad": normal_values(own_keys[4], (TOKENS, HEADS * DH), 1.0, 6.0, ((0, 16),)),
    }


def mixing(form, left, right):
    return jnp.einsum(form, left.astype(jnp.float32), right.astype(jnp.float32))

def features(inputs, weight):
    lifted = mixing('thd,hde->the', inputs, weight)
    mapped = jnp.where(lifted > 0, lifted + 1.0, jnp.exp(jnp.minimum(lifted, 0.0)))
    return (lifted, mapped.astype(jnp.bfloat16))

def slope_of(lifted):
    return jnp.where(lifted > 0, 1.0, jnp.exp(jnp.minimum(lifted, 0.0)))

def reference(queries, keys, values, feature_map, out_grad):
    block_count = TOKENS // TOK_DEV
    shaped = (block_count, TOK_DEV, HEADS, DH)
    query_blocks = queries.reshape(shaped)
    key_blocks = keys.reshape(shaped)
    value_blocks = values.reshape(shaped)
    grad_blocks = out_grad.reshape(shaped)
    token_ids = lax.broadcasted_iota(jnp.int32, (TOK_DEV, TOK_DEV), 0)
    other_ids = lax.broadcasted_iota(jnp.int32, (TOK_DEV, TOK_DEV), 1)
    causal = (token_ids >= other_ids)[None, :, :]
    zero_state = jnp.zeros((HEADS, DH, DH), jnp.float32)

    def forward_step(prefix, blocks):
        query_block, key_block, value_block = blocks
        lifted_q, feat_q = features(query_block, feature_map)
        lifted_k, feat_k = features(key_block, feature_map)
        scores = jnp.where(causal, mixing('the,she->hts', feat_q, feat_k), 0.0).astype(jnp.bfloat16)
        numerator = mixing('hts,shf->thf', scores, value_block) + mixing('the,hef->thf', feat_q, prefix.astype(jnp.bfloat16))
        recip = lax.rsqrt(lax.optimization_barrier(jnp.mean(numerator * numerator, axis=-1, keepdims=True)) + 1e-06)
        attended = (numerator * recip).astype(jnp.bfloat16)
        block_state = mixing('the,thf->hef', feat_k, value_block)
        return (prefix + block_state, (attended, prefix))
    last_state, (attended_blocks, prefixes) = lax.scan(forward_step, zero_state, (query_blocks, key_blocks, value_blocks))
    scale = 1.0 / math.sqrt(TOKENS)

    def backward_step(carry, blocks):
        suffix, weight_sum = carry
        query_block, key_block, value_block, grad_block, prefix = blocks
        lifted_q, feat_q = features(query_block, feature_map)
        lifted_k, feat_k = features(key_block, feature_map)
        prefix_low = prefix.astype(jnp.bfloat16)
        suffix_low = suffix.astype(jnp.bfloat16)
        scores = jnp.where(causal, mixing('the,she->hts', feat_q, feat_k), 0.0).astype(jnp.bfloat16)
        numerator = mixing('hts,shf->thf', scores, value_block) + mixing('the,hef->thf', feat_q, prefix_low)
        recip = lax.rsqrt(lax.optimization_barrier(jnp.mean(numerator * numerator, axis=-1, keepdims=True)) + 1e-06)
        upstream = grad_block.astype(jnp.float32)
        inner = lax.optimization_barrier(jnp.mean(upstream * numerator, axis=-1, keepdims=True))
        grad_numer = (recip * (upstream - numerator * recip * recip * inner)).astype(jnp.bfloat16)
        back_scores = jnp.where(causal, mixing('thf,shf->hts', grad_numer, value_block), 0.0).astype(jnp.bfloat16)
        grad_fq = mixing('hts,she->the', back_scores, feat_k) + mixing('thf,hef->the', grad_numer, prefix_low)
        grad_fk = mixing('hts,the->she', back_scores, feat_q) + mixing('shf,hef->she', value_block, suffix_low)
        value_grad = (mixing('hts,thf->shf', scores, grad_numer) + mixing('she,hef->shf', feat_k, suffix_low)).astype(jnp.bfloat16)
        grad_qa = (grad_fq * slope_of(lifted_q)).astype(jnp.bfloat16)
        grad_ka = (grad_fk * slope_of(lifted_k)).astype(jnp.bfloat16)
        query_grad = mixing('the,hde->thd', grad_qa, feature_map).astype(jnp.bfloat16)
        key_grad = mixing('the,hde->thd', grad_ka, feature_map).astype(jnp.bfloat16)
        weight_term = mixing('thd,the->hde', query_block, grad_qa) + mixing('thd,the->hde', key_block, grad_ka)
        local_adjoint = mixing('the,thf->hef', feat_q, grad_numer)
        return ((suffix + local_adjoint, weight_sum + weight_term), (query_grad, key_grad, value_grad))
    carry_end, (query_grads, key_grads, value_grads) = lax.scan(backward_step, (zero_state, zero_state), (query_blocks, key_blocks, value_blocks, grad_blocks, prefixes), reverse=True)
    flat = (TOKENS, HEADS * DH)
    feature_grad = (carry_end[1] * scale).reshape(HEADS * DH * DH)
    return (attended_blocks.reshape(flat), query_grads.reshape(flat), key_grads.reshape(flat), value_grads.reshape(flat), feature_grad)
```

```python
import functools
import math

import jax
import jax.numpy as jnp
from jax import lax
from jax.experimental import pallas as pl
from jax.experimental.pallas import tpu as pltpu
from jax.sharding import PartitionSpec as P

MESH = pl.DeviceIdType.MESH
BF16 = jnp.bfloat16
F32 = jnp.float32


def mm(a, b, ca, cb):
    return lax.dot_general(a, b, (((ca,), (cb,)), ((), ())), preferred_element_type=F32)


def kernel(n, heads, dh, scale, q_ref, k_ref, v_ref, w_ref, y_ref,
           att_ref, qg_ref, kg_ref, vg_ref, fg_ref,
           fq_s, fk_s, a_s, num_s, gfk_s, vgl_s, wt_s, g_s,
           u_send, u_recv, p_send, p_buf, r_send, r_recv, s_send, q_buf, f_send, f_recv,
           send_sems, recv_sems):
    me = lax.axis_index("seq")
    rows = heads * dh // n
    cph = n // heads
    tokens = q_ref.shape[0]
    my_head = me // cph

    barrier = pltpu.get_barrier_semaphore()

    @pl.loop(1, n)
    def _(i):
        pl.semaphore_signal(barrier, inc=1, device_id={"seq": lax.rem(me + i, n)}, device_id_type=MESH)

    causal = (lax.broadcasted_iota(jnp.int32, (tokens, tokens), 0)
              >= lax.broadcasted_iota(jnp.int32, (tokens, tokens), 1))

    def cols(h):
        return pl.ds(pl.multiple_of(h * dh, dh), dh)

    def chunks(h):
        return pl.ds(h * cph, cph)

    def remote(phase, src, dst, to):
        return pltpu.make_async_remote_copy(
            src_ref=src.at[to], dst_ref=dst.at[me], send_sem=send_sems.at[phase],
            recv_sem=recv_sems.at[phase, me], device_id={"seq": to}, device_id_type=MESH)

    def send_chunk(phase, src, dst, to):
        @pl.when(to != me)
        def _():
            remote(phase, src, dst, to).start()

        @pl.when(to == me)
        def _():
            dst[me] = src[me]

    def send_head(phase, src, dst, h):
        @pl.loop(0, cph)
        def _(c):
            send_chunk(phase, src, dst, h * cph + c)

    def wait_chunk(phase, dst, j):
        @pl.when(j != me)
        def _():
            pltpu.make_async_remote_copy(
                src_ref=dst.at[j], dst_ref=dst.at[j], send_sem=send_sems.at[phase],
                recv_sem=recv_sems.at[phase, j], device_id={"seq": j}, device_id_type=MESH).wait_recv()

    def wait_head(phase, dst, h):
        @pl.loop(0, cph)
        def _(c):
            wait_chunk(phase, dst, h * cph + c)

    def features(lifted):
        return jnp.where(lifted > 0, lifted + 1.0, jnp.exp(jnp.minimum(lifted, 0.0))).astype(BF16)

    def slope_of(feat):
        return jnp.minimum(feat.astype(F32), 1.0)

    def head_of(buf, h):
        return buf[chunks(h)].reshape(dh, dh)

    def put_head(buf, h, value):
        buf[chunks(h)] = value.astype(BF16).reshape(cph, rows, dh)

    def state(h):
        c = cols(h)
        feat = features(mm(k_ref[:, c], w_ref[h], 1, 0))
        fk_s[:, c] = feat
        put_head(u_send, h, mm(feat, v_ref[:, c], 0, 0))

    state(lax.rem(my_head + 1, heads))
    pl.semaphore_wait(barrier, n - 1)
    send_head(0, u_send, u_recv, lax.rem(my_head + 1, heads))

    @pl.loop(2, heads + 1)
    def _(i):
        h = lax.rem(my_head + i, heads)
        state(h)
        send_head(0, u_send, u_recv, h)

    @pl.loop(0, heads)
    def _(h):
        c = cols(h)
        feat = features(mm(q_ref[:, c], w_ref[h], 1, 0))
        fq_s[:, c] = feat
        score = jnp.where(causal, mm(feat, fk_s[:, c], 1, 1), 0.0).astype(BF16)
        a_s[h] = score
        num_s[:, c] = mm(score, v_ref[:, c], 1, 0)

    def scan_up(j, acc):
        wait_chunk(0, u_recv, j)
        p_send[j] = acc.astype(BF16)
        return acc + u_recv[j].astype(F32)

    lax.fori_loop(0, n, scan_up, jnp.zeros((rows, dh), F32))

    @pl.loop(1, n + 1)
    def _(i):
        send_chunk(1, p_send, p_buf, lax.rem(me + i, n))

    @pl.loop(0, heads)
    def _(i):
        h = lax.rem(my_head + heads - i, heads)
        c = cols(h)
        wait_head(1, p_buf, h)
        num = num_s[:, c] + mm(fq_s[:, c], head_of(p_buf, h), 1, 0)
        recip = lax.rsqrt(jnp.mean(num * num, axis=-1, keepdims=True) + 1e-06)
        att_ref[:, c] = (num * recip).astype(BF16)
        y = y_ref[:, c].astype(F32)
        inner = jnp.mean(y * num, axis=-1, keepdims=True)
        g = (recip * (y - num * (recip * recip * inner))).astype(BF16)
        g_s[:, c] = g
        put_head(r_send, h, mm(fq_s[:, c], g, 0, 0))
        send_head(2, r_send, r_recv, h)

    @pl.loop(0, heads)
    def _(h):
        c = cols(h)
        g = g_s[:, c]
        back = jnp.where(causal, mm(g, v_ref[:, c], 1, 1), 0.0).astype(BF16)
        fq = fq_s[:, c]
        gfq = mm(back, fk_s[:, c], 1, 0) + mm(g, head_of(p_buf, h), 1, 1)
        ga = (gfq * slope_of(fq)).astype(BF16)
        qg_ref[:, c] = mm(ga, w_ref[h], 1, 1).astype(BF16)
        wt_s[h] = mm(q_ref[:, c], ga, 0, 0)
        gfk_s[:, c] = mm(back, fq, 0, 0)
        vgl_s[:, c] = mm(a_s[h], g, 0, 0)

    def scan_down(i, acc):
        j = n - 1 - i
        wait_chunk(2, r_recv, j)
        s_send[j] = acc.astype(BF16)
        return acc + r_recv[j].astype(F32)

    lax.fori_loop(0, n, scan_down, jnp.zeros((rows, dh), F32))

    @pl.loop(1, n + 1)
    def _(i):
        send_chunk(3, s_send, q_buf, lax.rem(me + i, n))

    @pl.loop(0, heads)
    def _(i):
        h = lax.rem(my_head + heads - i, heads)
        c = cols(h)
        wait_head(3, q_buf, h)
        suffix = head_of(q_buf, h)
        fk = fk_s[:, c]
        vg_ref[:, c] = (vgl_s[:, c] + mm(fk, suffix, 1, 0)).astype(BF16)
        gfk = gfk_s[:, c] + mm(v_ref[:, c], suffix, 1, 1)
        gb = (gfk * slope_of(fk)).astype(BF16)
        kg_ref[:, c] = mm(gb, w_ref[h], 1, 1).astype(BF16)
        put_head(f_send, h, wt_s[h] + mm(k_ref[:, c], gb, 0, 0))
        send_head(4, f_send, f_recv, h)

    def collect(j, acc):
        wait_chunk(4, f_recv, j)
        return acc + f_recv[j].astype(F32)

    fg_ref[...] = lax.fori_loop(0, n, collect, jnp.zeros((rows, dh), F32)) * scale

    for phase, buf in enumerate((u_send, p_send, r_send, s_send, f_send)):
        part = buf.at[pl.ds(0, n - 1)]
        pltpu.make_async_remote_copy(
            src_ref=part, dst_ref=part, send_sem=send_sems.at[phase], recv_sem=recv_sems.at[phase, 0],
            device_id={"seq": lax.rem(me + 1, n)}, device_id_type=MESH).wait_send()


def local(queries, keys, values, feature_map, out_grad):
    tokens, width = queries.shape
    heads, dh, _ = feature_map.shape
    n = lax.axis_size("seq")
    rows = heads * dh // n
    wide = jax.ShapeDtypeStruct((tokens, width), BF16)
    vmem = pl.BlockSpec(memory_space=pltpu.VMEM)
    hold = pltpu.VMEM((n, rows, dh), BF16)
    outs = pl.pallas_call(
        functools.partial(kernel, n, heads, dh, 1.0 / math.sqrt(tokens * n)),
        out_shape=(wide, wide, wide, wide, jax.ShapeDtypeStruct((rows, dh), F32)),
        in_specs=[vmem] * 5,
        out_specs=(vmem,) * 5,
        scratch_shapes=[
            pltpu.VMEM((tokens, width), BF16),
            pltpu.VMEM((tokens, width), BF16),
            pltpu.VMEM((heads, tokens, tokens), BF16),
            pltpu.VMEM((tokens, width), F32),
            pltpu.VMEM((tokens, width), F32),
            pltpu.VMEM((tokens, width), F32),
            pltpu.VMEM((heads, dh, dh), F32),
            pltpu.VMEM((tokens, width), BF16),
        ] + [hold] * 10 + [
            pltpu.SemaphoreType.DMA((5,)),
            pltpu.SemaphoreType.DMA((5, n)),
        ],
        compiler_params=pltpu.CompilerParams(
            collective_id=0, has_side_effects=True, vmem_limit_bytes=48 << 20),
        name="linear_attention",
    )(queries, keys, values, feature_map, out_grad)
    return outs[:4] + (outs[4].reshape(rows * dh),)


def solution(mesh):
    wide = P(("grp", "seq"), None)
    return jax.shard_map(
        local, mesh=mesh, in_specs=(wide, wide, wide, P(), wide),
        out_specs=(wide, wide, wide, wide, P(("grp", "seq"))), check_vma=False)
```

```python
import functools
import math

import jax
import jax.numpy as jnp
from jax import lax
from jax.experimental import pallas as pl
from jax.experimental.pallas import tpu as pltpu
from jax.sharding import PartitionSpec as P

MESH = pl.DeviceIdType.MESH
BF16 = jnp.bfloat16
F32 = jnp.float32
GROUP = 4


def mm(a, b, ca, cb):
    return lax.dot_general(a, b, (((ca,), (cb,)), ((), ())), preferred_element_type=F32)


def kernel(n, heads, dh, scale, q_ref, k_ref, v_ref, w_ref, y_ref,
           att_ref, qg_ref, kg_ref, vg_ref, fg_ref,
           fq_s, fk_s, a_s, num_s, gfk_s, vgl_s, wt_s, g_s,
           u_send, r_send, f_send, p_full, s_full,
           u_pair, u_tot, u_recv, p_send, p_chip, p_fwd,
           r_pair, r_tot, r_recv, s_send, s_chip, s_fwd,
           f_pair, f_tot, f_recv,
           pair_send_sems, pair_recv_sems, chip_send_sems, chip_recv_sems):
    me = lax.axis_index("seq")
    chips = n // 2
    chip, core = me // 2, lax.rem(me, 2)
    other = 1 - core
    rows = heads * dh // n
    groups = heads // GROUP
    span = chips // groups
    my_group = chip // span
    tokens = q_ref.shape[0]
    wide = GROUP * dh
    first_core = core == 0

    barrier = pltpu.get_barrier_semaphore()

    @pl.loop(0, chips - 1)
    def _(i):
        to = 2 * lax.rem(chip + 1 + i, chips) + core
        pl.semaphore_signal(barrier, inc=1, device_id={"seq": to}, device_id_type=MESH)

    pl.semaphore_signal(barrier, inc=1, device_id={"seq": 2 * chip + other}, device_id_type=MESH)

    causal = (lax.broadcasted_iota(jnp.int32, (tokens, tokens), 0)
              >= lax.broadcasted_iota(jnp.int32, (tokens, tokens), 1))

    def cols(g):
        return [pl.ds(pl.multiple_of(g * wide + k * dh, dh), dh) for k in range(GROUP)]

    def part(g):
        return pl.ds(g * span, span)

    def to_pair(phase, g, src, dst):
        return pltpu.make_async_remote_copy(
            src_ref=src, dst_ref=dst, send_sem=pair_send_sems.at[phase],
            recv_sem=pair_recv_sems.at[phase, g], device_id={"seq": 2 * chip + other}, device_id_type=MESH)

    def send_chip(phase, src, dst, c):
        @pl.when(c != chip)
        def _():
            pltpu.make_async_remote_copy(
                src_ref=src.at[c], dst_ref=dst.at[chip], send_sem=chip_send_sems.at[phase],
                recv_sem=chip_recv_sems.at[phase, chip], device_id={"seq": 2 * c + core},
                device_id_type=MESH).start()

        @pl.when(c == chip)
        def _():
            dst[chip] = src[chip]

    def wait_chip(phase, dst, c):
        @pl.when(c != chip)
        def _():
            pltpu.make_async_remote_copy(
                src_ref=dst.at[c], dst_ref=dst.at[c], send_sem=chip_send_sems.at[phase],
                recv_sem=chip_recv_sems.at[phase, c], device_id={"seq": 2 * c + core},
                device_id_type=MESH).wait_recv()

    def send_group(phase, src, dst, g):
        @pl.loop(0, span)
        def _(i):
            send_chip(phase, src, dst, g * span + lax.rem(chip + i, span))

    def wait_group(phase, dst, g):
        @pl.loop(0, span)
        def _(i):
            wait_chip(phase, dst, g * span + i)

    def share(phase, g, full, paired, values):
        full[part(g)] = jnp.concatenate([v.astype(BF16) for v in values], axis=0).reshape(span, 2, rows, dh)
        to_pair(phase, g, full.at[part(g), other], paired.at[part(g)]).start()

    def total(phase, chip_phase, g, full, paired, tot, recv):
        to_pair(phase, g, paired.at[part(g)], paired.at[part(g)]).wait_recv()
        tot[part(g)] = (full[part(g), core].astype(F32) + paired[part(g)].astype(F32)).astype(BF16)
        send_group(chip_phase, tot, recv, g)

    def scan(phase, next_phase, recv, send, landing, order):
        def step(i, acc):
            c = order(i)
            wait_chip(phase, recv, c)
            send[c] = acc.astype(BF16)
            return acc + recv[c].astype(F32)

        lax.fori_loop(0, chips, step, jnp.zeros((rows, dh), F32))

        @pl.loop(0, groups)
        def _(i):
            send_group(next_phase, send, landing, lax.rem(my_group + i, groups))

    def hand_out(chip_phase, phase, g, landing, full, paired, fwd, out, own_adds):
        wait_group(chip_phase, landing, g)
        base = landing[part(g)].astype(F32)
        mine = base + jnp.where(own_adds, paired[part(g)].astype(F32), 0.0)
        theirs = base + jnp.where(own_adds, 0.0, full[part(g), core].astype(F32))
        fwd[part(g)] = theirs.astype(BF16)
        to_pair(phase, g, fwd.at[part(g)], out.at[part(g), core]).start()
        out[part(g), core] = mine.astype(BF16)

    def receive(phase, g, fwd, out):
        to_pair(phase, g, fwd.at[part(g)], out.at[part(g), other]).wait_recv()

    def heads_of(buf, g):
        block = buf[part(g)].reshape(wide, dh)
        return [block[k * dh:(k + 1) * dh] for k in range(GROUP)]

    def weights(g):
        return [w_ref[g * GROUP + k] for k in range(GROUP)]

    def features(lifted):
        return jnp.where(lifted > 0, lifted + 1.0, jnp.exp(jnp.minimum(lifted, 0.0))).astype(BF16)

    def slope_of(feat):
        return jnp.minimum(feat.astype(F32), 1.0)

    def state(g):
        cs = cols(g)
        lifted = [mm(k_ref[:, c], w, 1, 0) for c, w in zip(cs, weights(g))]
        feats = [features(x) for x in lifted]
        sums = [mm(f, v_ref[:, c], 0, 0) for c, f in zip(cs, feats)]
        for c, f in zip(cs, feats):
            fk_s[:, c] = f
        return sums

    def up(i):
        return lax.rem(my_group + i, groups)

    def down(i):
        return lax.rem(my_group + groups - i, groups)

    sums = state(up(1))
    pl.semaphore_wait(barrier, chips)
    share(0, up(1), u_send, u_pair, sums)

    @pl.loop(2, groups + 1)
    def _(i):
        share(0, up(i), u_send, u_pair, state(up(i)))
        total(0, 0, up(i - 1), u_send, u_pair, u_tot, u_recv)

    total(0, 0, up(groups), u_send, u_pair, u_tot, u_recv)

    def local_part(g):
        cs = cols(g)
        lifted = [mm(q_ref[:, c], w, 1, 0) for c, w in zip(cs, weights(g))]
        feats = [features(x) for x in lifted]
        scores = [mm(f, fk_s[:, c], 1, 1) for c, f in zip(cs, feats)]
        scores = [jnp.where(causal, x, 0.0).astype(BF16) for x in scores]
        nums = [mm(x, v_ref[:, c], 1, 0) for c, x in zip(cs, scores)]
        for k, c in enumerate(cs):
            fq_s[:, c] = feats[k]
            a_s[g * GROUP + k] = scores[k]
            num_s[:, c] = nums[k]

    half = groups // 2
    pl.loop(0, half)(local_part)
    scan(0, 1, u_recv, p_send, p_chip, lambda i: i)
    pl.loop(half, groups)(local_part)

    hand_out(1, 1, down(0), p_chip, u_send, u_pair, p_fwd, p_full, core == 1)

    @pl.loop(0, groups)
    def _(i):
        @pl.when(i + 1 < groups)
        def _():
            hand_out(1, 1, down(i + 1), p_chip, u_send, u_pair, p_fwd, p_full, core == 1)

        g = down(i)
        cs = cols(g)
        receive(1, g, p_fwd, p_full)
        prefixes = heads_of(p_full, g)
        fqs = [fq_s[:, c] for c in cs]
        nums = [num_s[:, c] + mm(f, p, 1, 0) for c, f, p in zip(cs, fqs, prefixes)]
        recips = [lax.rsqrt(jnp.mean(x * x, axis=-1, keepdims=True) + 1e-06) for x in nums]
        ys = [y_ref[:, c].astype(F32) for c in cs]
        inners = [jnp.mean(y * x, axis=-1, keepdims=True) for y, x in zip(ys, nums)]
        grads = [(r * (y - x * (r * r * m))).astype(BF16) for r, y, x, m in zip(recips, ys, nums, inners)]
        sums = [mm(f, x, 0, 0) for f, x in zip(fqs, grads)]
        for c, x, r, gr in zip(cs, nums, recips, grads):
            att_ref[:, c] = (x * r).astype(BF16)
            g_s[:, c] = gr
        share(2, g, r_send, r_pair, sums)

        @pl.when(i > 0)
        def _():
            total(2, 2, down(i - 1), r_send, r_pair, r_tot, r_recv)

    total(2, 2, down(groups - 1), r_send, r_pair, r_tot, r_recv)

    def adjoint_part(g):
        cs = cols(g)
        grads = [g_s[:, c] for c in cs]
        ws = weights(g)
        prefixes = heads_of(p_full, g)
        backs = [mm(x, v_ref[:, c], 1, 1) for x, c in zip(grads, cs)]
        backs = [jnp.where(causal, x, 0.0).astype(BF16) for x in backs]
        gfqs = [mm(b, fk_s[:, c], 1, 0) + mm(x, p, 1, 1) for b, c, x, p in zip(backs, cs, grads, prefixes)]
        fqs = [fq_s[:, c] for c in cs]
        gas = [(x * slope_of(f)).astype(BF16) for x, f in zip(gfqs, fqs)]
        qgs = [mm(x, w, 1, 1).astype(BF16) for x, w in zip(gas, ws)]
        wts = [mm(q_ref[:, c], x, 0, 0) for c, x in zip(cs, gas)]
        gfks = [mm(b, f, 0, 0) for b, f in zip(backs, fqs)]
        vgls = [mm(a_s[g * GROUP + k], x, 0, 0) for k, x in enumerate(grads)]
        for k, c in enumerate(cs):
            qg_ref[:, c] = qgs[k]
            wt_s[g * GROUP + k] = wts[k]
            gfk_s[:, c] = gfks[k]
            vgl_s[:, c] = vgls[k]

    pl.loop(0, half)(adjoint_part)
    scan(2, 3, r_recv, s_send, s_chip, lambda i: chips - 1 - i)
    pl.loop(half, groups)(adjoint_part)

    hand_out(3, 3, down(0), s_chip, r_send, r_pair, s_fwd, s_full, first_core)

    @pl.loop(0, groups)
    def _(i):
        @pl.when(i + 1 < groups)
        def _():
            hand_out(3, 3, down(i + 1), s_chip, r_send, r_pair, s_fwd, s_full, first_core)

        g = down(i)
        cs = cols(g)
        receive(3, g, s_fwd, s_full)
        ws = weights(g)
        suffixes = heads_of(s_full, g)
        fks = [fk_s[:, c] for c in cs]
        gfks = [gfk_s[:, c] + mm(v_ref[:, c], s, 1, 1) for c, s in zip(cs, suffixes)]
        gbs = [(x * slope_of(f)).astype(BF16) for x, f in zip(gfks, fks)]
        wts = [wt_s[g * GROUP + k] + mm(k_ref[:, c], x, 0, 0) for k, (c, x) in enumerate(zip(cs, gbs))]
        share(4, g, f_send, f_pair, wts)
        vgs = [vgl_s[:, c] + mm(f, s, 1, 0) for c, f, s in zip(cs, fks, suffixes)]
        kgs = [mm(x, w, 1, 1) for x, w in zip(gbs, ws)]
        for c, a, b in zip(cs, vgs, kgs):
            vg_ref[:, c] = a.astype(BF16)
            kg_ref[:, c] = b.astype(BF16)
        total(4, 4, g, f_send, f_pair, f_tot, f_recv)

    def collect(c, acc):
        wait_chip(4, f_recv, c)
        return acc + f_recv[c].astype(F32)

    fg_ref[...] = lax.fori_loop(0, chips, collect, jnp.zeros((rows, dh), F32)) * scale

    for phase, buf in enumerate((u_tot, p_send, r_tot, s_send, f_tot)):
        some = buf.at[pl.ds(0, chips - 1)]
        pltpu.make_async_remote_copy(
            src_ref=some, dst_ref=some, send_sem=chip_send_sems.at[phase], recv_sem=chip_recv_sems.at[phase, 0],
            device_id={"seq": 2 * chip + other}, device_id_type=MESH).wait_send()
        to_pair(phase, 0, buf, buf).wait_send()


def local(queries, keys, values, feature_map, out_grad):
    tokens, width = queries.shape
    heads, dh, _ = feature_map.shape
    n = lax.axis_size("seq")
    chips, groups = n // 2, heads // GROUP
    rows = heads * dh // n
    wide = jax.ShapeDtypeStruct((tokens, width), BF16)
    vmem = pl.BlockSpec(memory_space=pltpu.VMEM)
    outs = pl.pallas_call(
        functools.partial(kernel, n, heads, dh, 1.0 / math.sqrt(tokens * n)),
        out_shape=(wide, wide, wide, wide, jax.ShapeDtypeStruct((rows, dh), F32)),
        in_specs=[vmem] * 5,
        out_specs=(vmem,) * 5,
        scratch_shapes=[
            pltpu.VMEM((tokens, width), BF16),
            pltpu.VMEM((tokens, width), BF16),
            pltpu.VMEM((heads, tokens, tokens), BF16),
            pltpu.VMEM((tokens, width), F32),
            pltpu.VMEM((tokens, width), F32),
            pltpu.VMEM((tokens, width), F32),
            pltpu.VMEM((heads, dh, dh), F32),
            pltpu.VMEM((tokens, width), BF16),
        ] + [pltpu.VMEM((chips, 2, rows, dh), BF16)] * 5 + [pltpu.VMEM((chips, rows, dh), BF16)] * 15 + [
            pltpu.SemaphoreType.DMA((5,)),
            pltpu.SemaphoreType.DMA((5, groups)),
            pltpu.SemaphoreType.DMA((5,)),
            pltpu.SemaphoreType.DMA((5, chips)),
        ],
        compiler_params=pltpu.CompilerParams(
            collective_id=0, has_side_effects=True, vmem_limit_bytes=48 << 20),
        name="linear_attention",
    )(queries, keys, values, feature_map, out_grad)
    return outs[:4] + (outs[4].reshape(rows * dh),)


def solution(mesh):
    wide = P(("grp", "seq"), None)
    return jax.shard_map(
        local, mesh=mesh, in_specs=(wide, wide, wide, P(), wide),
        out_specs=(wide, wide, wide, wide, P(("grp", "seq"))), check_vma=False)
```

```python
import functools
import math

import jax
import jax.numpy as jnp
from jax import lax
from jax.experimental import pallas as pl
from jax.experimental.pallas import tpu as pltpu
from jax.sharding import PartitionSpec as P

MESH = pl.DeviceIdType.MESH
BF16 = jnp.bfloat16
F32 = jnp.float32
GROUP = 4
PIECES = 2


def mm(a, b, ca, cb):
    return lax.dot_general(a, b, (((ca,), (cb,)), ((), ())), preferred_element_type=F32)


def kernel(n, heads, dh, scale, q_hbm, k_hbm, v_hbm, w_hbm, y_hbm,
           att_hbm, qg_hbm, kg_hbm, vg_hbm, fg_ref,
           q_ref, k_ref, v_ref, w_ref, y_ref, att_ref, qg_ref, kg_ref, vg_ref,
           fq_s, fk_s, gb_s, a_s, num_s, gfk_s, vgl_s, wt_s, g_s,
           u_send, r_send, f_send, p_full, s_full,
           u_pair, u_tot, u_recv, p_send, p_chip, p_fwd,
           r_pair, r_tot, r_recv, s_send, s_chip, s_fwd,
           f_pair, f_tot, f_recv,
           pair_send_sems, pair_recv_sems, chip_send_sems, chip_recv_sems, load_sems, late_sems, out_sems):
    me = lax.axis_index("seq")
    chips = n // 2
    chip, core = me // 2, lax.rem(me, 2)
    other = 1 - core
    rows = heads * dh // n
    groups = heads // GROUP
    span = chips // groups
    my_group = chip // span
    tokens = q_ref.shape[0]
    wide = GROUP * dh

    def loads(g):
        some = pl.ds(pl.multiple_of(g * wide, wide), wide)
        some_heads = pl.ds(g * GROUP, GROUP)
        return (
            pltpu.make_async_copy(w_hbm.at[some_heads], w_ref.at[some_heads], load_sems.at[0, g]),
            pltpu.make_async_copy(k_hbm.at[:, some], k_ref.at[:, some], load_sems.at[1, g]),
            pltpu.make_async_copy(v_hbm.at[:, some], v_ref.at[:, some], load_sems.at[2, g]),
        )

    def store(which, g):
        some = pl.ds(pl.multiple_of(g * wide, wide), wide)
        src, dst = ((att_ref, att_hbm), (qg_ref, qg_hbm), (kg_ref, kg_hbm), (vg_ref, vg_hbm))[which]
        return pltpu.make_async_copy(src.at[:, some], dst.at[:, some], out_sems.at[which, g])

    @pl.loop(1, groups + 1)
    def _(i):
        for copy in loads(lax.rem(my_group + i, groups)):
            copy.start()

    load_q = pltpu.make_async_copy(q_hbm, q_ref, late_sems.at[0])
    load_y = pltpu.make_async_copy(y_hbm, y_ref, late_sems.at[1])
    load_q.start()
    load_y.start()
    first_core = core == 0

    barrier = pltpu.get_barrier_semaphore()

    @pl.loop(0, chips - 1)
    def _(i):
        to = 2 * lax.rem(chip + 1 + i, chips) + core
        pl.semaphore_signal(barrier, inc=1, device_id={"seq": to}, device_id_type=MESH)

    pl.semaphore_signal(barrier, inc=1, device_id={"seq": 2 * chip + other}, device_id_type=MESH)

    causal = (lax.broadcasted_iota(jnp.int32, (tokens, tokens), 0)
              >= lax.broadcasted_iota(jnp.int32, (tokens, tokens), 1))

    def cols(g):
        return [pl.ds(pl.multiple_of(g * wide + k * dh, dh), dh) for k in range(GROUP)]

    def part(g):
        return pl.ds(g * span, span)

    def to_pair(phase, g, src, dst):
        return pltpu.make_async_remote_copy(
            src_ref=src, dst_ref=dst, send_sem=pair_send_sems.at[phase],
            recv_sem=pair_recv_sems.at[phase, g], device_id={"seq": 2 * chip + other}, device_id_type=MESH)

    def send_chip(phase, src, dst, c):
        @pl.when(c != chip)
        def _():
            pltpu.make_async_remote_copy(
                src_ref=src.at[c], dst_ref=dst.at[chip], send_sem=chip_send_sems.at[phase],
                recv_sem=chip_recv_sems.at[phase, chip], device_id={"seq": 2 * c + core},
                device_id_type=MESH).start()

        @pl.when(c == chip)
        def _():
            dst[chip] = src[chip]

    def wait_chip(phase, dst, c):
        @pl.when(c != chip)
        def _():
            pltpu.make_async_remote_copy(
                src_ref=dst.at[c], dst_ref=dst.at[c], send_sem=chip_send_sems.at[phase],
                recv_sem=chip_recv_sems.at[phase, c], device_id={"seq": 2 * c + core},
                device_id_type=MESH).wait_recv()

    def send_group(phase, src, dst, g):
        @pl.loop(0, span)
        def _(i):
            send_chip(phase, src, dst, g * span + lax.rem(chip + i, span))

    def wait_group(phase, dst, g):
        @pl.loop(0, span)
        def _(i):
            wait_chip(phase, dst, g * span + i)

    def share(phase, g, full, paired, values):
        full[part(g)] = jnp.concatenate([v.astype(BF16) for v in values], axis=0).reshape(span, 2, rows, dh)
        to_pair(phase, g, full.at[part(g), other], paired.at[part(g)]).start()

    def total(phase, chip_phase, g, full, paired, tot, recv):
        to_pair(phase, g, paired.at[part(g)], paired.at[part(g)]).wait_recv()
        tot[part(g)] = (full[part(g), core].astype(F32) + paired[part(g)].astype(F32)).astype(BF16)
        send_group(chip_phase, tot, recv, g)

    def scan(phase, next_phase, recv, send, landing, order):
        def step(i, acc):
            c = order(i)
            wait_chip(phase, recv, c)
            send[c] = acc.astype(BF16)
            return acc + recv[c].astype(F32)

        lax.fori_loop(0, chips, step, jnp.zeros((rows, dh), F32))

        @pl.loop(0, groups)
        def _(i):
            send_group(next_phase, send, landing, lax.rem(my_group + i, groups))

    def hand_out(chip_phase, phase, g, landing, full, paired, fwd, out, own_adds):
        wait_group(chip_phase, landing, g)
        base = landing[part(g)].astype(F32)
        mine = base + jnp.where(own_adds, paired[part(g)].astype(F32), 0.0)
        theirs = base + jnp.where(own_adds, 0.0, full[part(g), core].astype(F32))
        fwd[part(g)] = theirs.astype(BF16)
        to_pair(phase, g, fwd.at[part(g)], out.at[part(g), core]).start()
        out[part(g), core] = mine.astype(BF16)

    def receive(phase, g, fwd, out):
        to_pair(phase, g, fwd.at[part(g)], out.at[part(g), other]).wait_recv()

    def heads_of(buf, g):
        block = buf[part(g)].reshape(wide, dh)
        return [block[k * dh:(k + 1) * dh] for k in range(GROUP)]

    def weights(g):
        return [w_ref[g * GROUP + k] for k in range(GROUP)]

    def features(lifted):
        return jnp.where(lifted > 0, lifted + 1.0, jnp.exp(jnp.minimum(lifted, 0.0))).astype(BF16)

    def slope_of(feat):
        return jnp.minimum(feat.astype(F32), 1.0)

    def state(g):
        for copy in loads(g):
            copy.wait()
        cs = cols(g)
        lifted = [mm(k_ref[:, c], w, 1, 0) for c, w in zip(cs, weights(g))]
        feats = [features(x) for x in lifted]
        sums = [mm(f, v_ref[:, c], 0, 0) for c, f in zip(cs, feats)]
        for c, f in zip(cs, feats):
            fk_s[:, c] = f
        return sums

    def up(i):
        return lax.rem(my_group + i, groups)

    def down(i):
        return lax.rem(my_group + groups - i, groups)

    sums = state(up(1))
    pl.semaphore_wait(barrier, chips)
    share(0, up(1), u_send, u_pair, sums)

    @pl.loop(2, groups + 1)
    def _(i):
        share(0, up(i), u_send, u_pair, state(up(i)))
        total(0, 0, up(i - 1), u_send, u_pair, u_tot, u_recv)

    total(0, 0, up(groups), u_send, u_pair, u_tot, u_recv)

    def local_part(g):
        cs = cols(g)
        lifted = [mm(q_ref[:, c], w, 1, 0) for c, w in zip(cs, weights(g))]
        feats = [features(x) for x in lifted]
        scores = [mm(f, fk_s[:, c], 1, 1) for c, f in zip(cs, feats)]
        scores = [jnp.where(causal, x, 0.0).astype(BF16) for x in scores]
        nums = [mm(x, v_ref[:, c], 1, 0) for c, x in zip(cs, scores)]
        for k, c in enumerate(cs):
            fq_s[:, c] = feats[k]
            a_s[g * GROUP + k] = scores[k]
            num_s[:, c] = nums[k]

    half = groups // 2
    load_q.wait()
    pl.loop(0, half)(local_part)
    scan(0, 1, u_recv, p_send, p_chip, lambda i: i)
    pl.loop(half, groups)(local_part)

    load_y.wait()
    hand_out(1, 1, down(0), p_chip, u_send, u_pair, p_fwd, p_full, core == 1)

    @pl.loop(0, groups)
    def _(i):
        @pl.when(i + 1 < groups)
        def _():
            hand_out(1, 1, down(i + 1), p_chip, u_send, u_pair, p_fwd, p_full, core == 1)

        g = down(i)
        cs = cols(g)
        receive(1, g, p_fwd, p_full)
        prefixes = heads_of(p_full, g)
        fqs = [fq_s[:, c] for c in cs]
        nums = [num_s[:, c] + mm(f, p, 1, 0) for c, f, p in zip(cs, fqs, prefixes)]
        recips = [lax.rsqrt(jnp.mean(x * x, axis=-1, keepdims=True) + 1e-06) for x in nums]
        ys = [y_ref[:, c].astype(F32) for c in cs]
        inners = [jnp.mean(y * x, axis=-1, keepdims=True) for y, x in zip(ys, nums)]
        grads = [(r * (y - x * (r * r * m))).astype(BF16) for r, y, x, m in zip(recips, ys, nums, inners)]
        sums = [mm(f, x, 0, 0) for f, x in zip(fqs, grads)]
        for c, x, r, gr in zip(cs, nums, recips, grads):
            att_ref[:, c] = (x * r).astype(BF16)
            g_s[:, c] = gr
        store(0, g).start()
        share(2, g, r_send, r_pair, sums)

        @pl.when(i > 0)
        def _():
            total(2, 2, down(i - 1), r_send, r_pair, r_tot, r_recv)

    total(2, 2, down(groups - 1), r_send, r_pair, r_tot, r_recv)

    def adjoint_part(g):
        cs = cols(g)
        grads = [g_s[:, c] for c in cs]
        ws = weights(g)
        prefixes = heads_of(p_full, g)
        backs = [mm(x, v_ref[:, c], 1, 1) for x, c in zip(grads, cs)]
        backs = [jnp.where(causal, x, 0.0).astype(BF16) for x in backs]
        gfqs = [mm(b, fk_s[:, c], 1, 0) + mm(x, p, 1, 1) for b, c, x, p in zip(backs, cs, grads, prefixes)]
        fqs = [fq_s[:, c] for c in cs]
        gas = [(x * slope_of(f)).astype(BF16) for x, f in zip(gfqs, fqs)]
        qgs = [mm(x, w, 1, 1).astype(BF16) for x, w in zip(gas, ws)]
        wts = [mm(q_ref[:, c], x, 0, 0) for c, x in zip(cs, gas)]
        gfks = [mm(b, f, 0, 0) for b, f in zip(backs, fqs)]
        vgls = [mm(a_s[g * GROUP + k], x, 0, 0) for k, x in enumerate(grads)]
        for k, c in enumerate(cs):
            qg_ref[:, c] = qgs[k]
            wt_s[g * GROUP + k] = wts[k]
            gfk_s[:, c] = gfks[k]
            vgl_s[:, c] = vgls[k]
        store(1, g).start()

    pl.loop(0, half)(adjoint_part)
    scan(2, 3, r_recv, s_send, s_chip, lambda i: chips - 1 - i)
    pl.loop(half, groups)(adjoint_part)

    hand_out(3, 3, down(0), s_chip, r_send, r_pair, s_fwd, s_full, first_core)

    @pl.loop(0, groups)
    def _(i):
        @pl.when(i + 1 < groups)
        def _():
            hand_out(3, 3, down(i + 1), s_chip, r_send, r_pair, s_fwd, s_full, first_core)

        g = down(i)
        cs = cols(g)
        receive(3, g, s_fwd, s_full)
        suffixes = heads_of(s_full, g)
        fks = [fk_s[:, c] for c in cs]
        gfks = [gfk_s[:, c] + mm(v_ref[:, c], s, 1, 1) for c, s in zip(cs, suffixes)]
        gbs = [(x * slope_of(f)).astype(BF16) for x, f in zip(gfks, fks)]
        wts = [wt_s[g * GROUP + k] + mm(k_ref[:, c], x, 0, 0) for k, (c, x) in enumerate(zip(cs, gbs))]
        for c, x in zip(cs, gbs):
            gb_s[:, c] = x
        share(4, g, f_send, f_pair, wts)

        @pl.when(i > 0)
        def _():
            total(4, 4, down(i - 1), f_send, f_pair, f_tot, f_recv)

    total(4, 4, down(groups - 1), f_send, f_pair, f_tot, f_recv)

    @pl.loop(0, groups)
    def _(g):
        cs = cols(g)
        suffixes = heads_of(s_full, g)
        vgs = [vgl_s[:, c] + mm(fk_s[:, c], s, 1, 0) for c, s in zip(cs, suffixes)]
        kgs = [mm(gb_s[:, c], w, 1, 1) for c, w in zip(cs, weights(g))]
        for c, a, b in zip(cs, vgs, kgs):
            vg_ref[:, c] = a.astype(BF16)
            kg_ref[:, c] = b.astype(BF16)
        store(2, g).start()
        store(3, g).start()

    def collect(c, acc):
        wait_chip(4, f_recv, c)
        return acc + f_recv[c].astype(F32)

    fg_ref[...] = lax.fori_loop(0, chips, collect, jnp.zeros((rows, dh), F32)) * scale

    @pl.loop(0, groups)
    def _(g):
        for which in range(4):
            store(which, g).wait()

    for phase, buf in enumerate((u_tot, p_send, r_tot, s_send, f_tot)):
        some = buf.at[pl.ds(0, chips - 1)]
        pltpu.make_async_remote_copy(
            src_ref=some, dst_ref=some, send_sem=chip_send_sems.at[phase], recv_sem=chip_recv_sems.at[phase, 0],
            device_id={"seq": 2 * chip + other}, device_id_type=MESH).wait_send()
        to_pair(phase, 0, buf, buf).wait_send()


def copy_out(*refs):
    ins, outs, held = refs[:5], refs[5:10], refs[10:15]
    in_sems, out_sems = refs[15:]

    def parts(sources, targets, sems):
        copies = []
        for i, (source, target) in enumerate(zip(sources, targets)):
            size = source.shape[0] // PIECES
            for p in range(PIECES):
                some = pl.ds(p * size, size)
                copies.append(pltpu.make_async_copy(source.at[some], target.at[some], sems.at[i, p]))
        return copies

    reads = parts(ins, held, in_sems)
    writes = parts(held, outs, out_sems)
    for read in reads:
        read.start()
    for read, write in zip(reads, writes):
        read.wait()
        write.start()
    for write in writes:
        write.wait()


def local(queries, keys, values, feature_map, out_grad):
    tokens, width = queries.shape
    heads, dh, _ = feature_map.shape
    n = lax.axis_size("seq")
    chips, groups = n // 2, heads // GROUP
    rows = heads * dh // n
    wide = jax.ShapeDtypeStruct((tokens, width), BF16)
    vmem = pl.BlockSpec(memory_space=pltpu.VMEM)
    hbm = pl.BlockSpec(memory_space=pltpu.HBM)
    shapes = (wide, wide, wide, wide, jax.ShapeDtypeStruct((rows, dh), F32))
    outs = pl.pallas_call(
        functools.partial(kernel, n, heads, dh, 1.0 / math.sqrt(tokens * n)),
        out_shape=shapes,
        in_specs=[hbm] * 5,
        out_specs=(hbm,) * 4 + (vmem,),
        scratch_shapes=[pltpu.VMEM((tokens, width), BF16)] * 3 + [pltpu.VMEM((heads, dh, dh), BF16)] + [
            pltpu.VMEM((tokens, width), BF16)] * 8 + [
            pltpu.VMEM((heads, tokens, tokens), BF16),
            pltpu.VMEM((tokens, width), F32),
            pltpu.VMEM((tokens, width), F32),
            pltpu.VMEM((tokens, width), F32),
            pltpu.VMEM((heads, dh, dh), F32),
            pltpu.VMEM((tokens, width), BF16),
        ] + [pltpu.VMEM((chips, 2, rows, dh), BF16)] * 5 + [pltpu.VMEM((chips, rows, dh), BF16)] * 15 + [
            pltpu.SemaphoreType.DMA((5,)),
            pltpu.SemaphoreType.DMA((5, groups)),
            pltpu.SemaphoreType.DMA((5,)),
            pltpu.SemaphoreType.DMA((5, chips)),
            pltpu.SemaphoreType.DMA((3, groups)),
            pltpu.SemaphoreType.DMA((2,)),
            pltpu.SemaphoreType.DMA((4, groups)),
        ],
        compiler_params=pltpu.CompilerParams(
            collective_id=0, has_side_effects=True, vmem_limit_bytes=56 << 20),
        name="linear_attention",
    )(queries, keys, values, feature_map, out_grad)
    outs = pl.pallas_call(
        copy_out,
        out_shape=shapes,
        in_specs=[hbm] * 5,
        out_specs=(hbm,) * 5,
        scratch_shapes=[pltpu.VMEM(x.shape, x.dtype) for x in shapes] + [pltpu.SemaphoreType.DMA((5, PIECES))] * 2,
        compiler_params=pltpu.CompilerParams(vmem_limit_bytes=56 << 20),
        name="copy_out",
    )(*outs)
    return tuple(outs[:4]) + (outs[4].reshape(rows * dh),)


def solution(mesh):
    wide = P(("grp", "seq"), None)
    return jax.shard_map(
        local, mesh=mesh, in_specs=(wide, wide, wide, P(), wide),
        out_specs=(wide, wide, wide, wide, P(("grp", "seq"))), check_vma=False)
```

```python
import functools
import math

import jax
import jax.numpy as jnp
from jax import lax
from jax.experimental import pallas as pl
from jax.experimental.pallas import tpu as pltpu
from jax.sharding import PartitionSpec as P

MESH = pl.DeviceIdType.MESH
BF16 = jnp.bfloat16
F32 = jnp.float32
GROUP = 4
PIECES = 1


def mm(a, b, ca, cb):
    return lax.dot_general(a, b, (((ca,), (cb,)), ((), ())), preferred_element_type=F32)


def kernel(n, heads, dh, scale, q_hbm, k_hbm, v_hbm, w_hbm, y_hbm,
           att_hbm, qg_hbm, kg_hbm, vg_hbm, fg_ref,
           q_ref, k_ref, v_ref, w_ref, y_ref, att_ref, qg_ref, kg_ref, vg_ref,
           fq_s, fk_s, gb_s, a_s, num_s, gfk_s, vgl_s, wt_s, g_s,
           u_send, r_send, f_send, p_full, s_full,
           u_pair, u_tot, u_recv, p_send, p_chip, p_fwd,
           r_pair, r_tot, r_recv, s_send, s_chip, s_fwd,
           f_pair, f_tot, f_recv,
           pair_send_sems, pair_recv_sems, chip_send_sems, chip_recv_sems, load_sems, late_sems, out_sems):
    me = lax.axis_index("seq")
    chips = n // 2
    chip, core = me // 2, lax.rem(me, 2)
    other = 1 - core
    rows = heads * dh // n
    groups = heads // GROUP
    span = chips // groups
    my_group = chip // span
    tokens = q_ref.shape[0]
    wide = GROUP * dh

    def loads(g):
        some = pl.ds(pl.multiple_of(g * wide, wide), wide)
        some_heads = pl.ds(g * GROUP, GROUP)
        return (
            pltpu.make_async_copy(w_hbm.at[some_heads], w_ref.at[some_heads], load_sems.at[0, g]),
            pltpu.make_async_copy(k_hbm.at[:, some], k_ref.at[:, some], load_sems.at[1, g]),
            pltpu.make_async_copy(v_hbm.at[:, some], v_ref.at[:, some], load_sems.at[2, g]),
        )

    def store(which, g):
        some = pl.ds(pl.multiple_of(g * wide, wide), wide)
        src, dst = ((att_ref, att_hbm), (qg_ref, qg_hbm), (kg_ref, kg_hbm), (vg_ref, vg_hbm))[which]
        return pltpu.make_async_copy(src.at[:, some], dst.at[:, some], out_sems.at[which, g])

    @pl.loop(1, groups + 1)
    def _(i):
        for copy in loads(lax.rem(my_group + i, groups)):
            copy.start()

    load_q = pltpu.make_async_copy(q_hbm, q_ref, late_sems.at[0])
    load_y = pltpu.make_async_copy(y_hbm, y_ref, late_sems.at[1])
    load_q.start()
    load_y.start()
    first_core = core == 0

    barrier = pltpu.get_barrier_semaphore()

    @pl.loop(0, chips - 1)
    def _(i):
        to = 2 * lax.rem(chip + 1 + i, chips) + core
        pl.semaphore_signal(barrier, inc=1, device_id={"seq": to}, device_id_type=MESH)

    pl.semaphore_signal(barrier, inc=1, device_id={"seq": 2 * chip + other}, device_id_type=MESH)

    causal = (lax.broadcasted_iota(jnp.int32, (tokens, tokens), 0)
              >= lax.broadcasted_iota(jnp.int32, (tokens, tokens), 1))

    def cols(g):
        return [pl.ds(pl.multiple_of(g * wide + k * dh, dh), dh) for k in range(GROUP)]

    def part(g):
        return pl.ds(g * span, span)

    def to_pair(phase, g, src, dst):
        return pltpu.make_async_remote_copy(
            src_ref=src, dst_ref=dst, send_sem=pair_send_sems.at[phase],
            recv_sem=pair_recv_sems.at[phase, g], device_id={"seq": 2 * chip + other}, device_id_type=MESH)

    def send_chip(phase, src, dst, c):
        @pl.when(c != chip)
        def _():
            pltpu.make_async_remote_copy(
                src_ref=src.at[c], dst_ref=dst.at[chip], send_sem=chip_send_sems.at[phase],
                recv_sem=chip_recv_sems.at[phase, chip], device_id={"seq": 2 * c + core},
                device_id_type=MESH).start()

        @pl.when(c == chip)
        def _():
            dst[chip] = src[chip]

    def wait_chip(phase, dst, c):
        @pl.when(c != chip)
        def _():
            pltpu.make_async_remote_copy(
                src_ref=dst.at[c], dst_ref=dst.at[c], send_sem=chip_send_sems.at[phase],
                recv_sem=chip_recv_sems.at[phase, c], device_id={"seq": 2 * c + core},
                device_id_type=MESH).wait_recv()

    def send_group(phase, src, dst, g):
        @pl.loop(0, span, unroll=span <= 8)
        def _(i):
            send_chip(phase, src, dst, g * span + lax.rem(chip + i, span))

    def wait_group(phase, dst, g):
        @pl.loop(0, span, unroll=span <= 8)
        def _(i):
            wait_chip(phase, dst, g * span + i)

    def share(phase, g, full, paired, values):
        full[part(g)] = jnp.concatenate([v.astype(BF16) for v in values], axis=0).reshape(span, 2, rows, dh)
        to_pair(phase, g, full.at[part(g), other], paired.at[part(g)]).start()

    def total(phase, chip_phase, g, full, paired, tot, recv):
        to_pair(phase, g, paired.at[part(g)], paired.at[part(g)]).wait_recv()
        tot[part(g)] = (full[part(g), core].astype(F32) + paired[part(g)].astype(F32)).astype(BF16)
        send_group(chip_phase, tot, recv, g)

    def scan(phase, next_phase, recv, send, landing, order):
        def step(i, acc):
            c = order(i)
            wait_chip(phase, recv, c)
            send[c] = acc.astype(BF16)
            return acc + recv[c].astype(F32)

        lax.fori_loop(0, chips, step, jnp.zeros((rows, dh), F32), unroll=chips <= 8)

        @pl.loop(0, groups, unroll=chips <= 8)
        def _(i):
            send_group(next_phase, send, landing, lax.rem(my_group + i, groups))

    def hand_out(chip_phase, phase, g, landing, full, paired, fwd, out, own_adds):
        wait_group(chip_phase, landing, g)
        base = landing[part(g)].astype(F32)
        mine = base + jnp.where(own_adds, paired[part(g)].astype(F32), 0.0)
        theirs = base + jnp.where(own_adds, 0.0, full[part(g), core].astype(F32))
        fwd[part(g)] = theirs.astype(BF16)
        to_pair(phase, g, fwd.at[part(g)], out.at[part(g), core]).start()
        out[part(g), core] = mine.astype(BF16)

    def receive(phase, g, fwd, out):
        to_pair(phase, g, fwd.at[part(g)], out.at[part(g), other]).wait_recv()

    def heads_of(buf, g):
        block = buf[part(g)].reshape(wide, dh)
        return [block[k * dh:(k + 1) * dh] for k in range(GROUP)]

    def weights(g):
        return [w_ref[g * GROUP + k] for k in range(GROUP)]

    def features(lifted):
        return jnp.where(lifted > 0, lifted + 1.0, jnp.exp(jnp.minimum(lifted, 0.0))).astype(BF16)

    def slope_of(feat):
        return jnp.minimum(feat.astype(F32), 1.0)

    def state(g):
        for copy in loads(g):
            copy.wait()
        cs = cols(g)
        lifted = [mm(k_ref[:, c], w, 1, 0) for c, w in zip(cs, weights(g))]
        feats = [features(x) for x in lifted]
        sums = [mm(f, v_ref[:, c], 0, 0) for c, f in zip(cs, feats)]
        for c, f in zip(cs, feats):
            fk_s[:, c] = f
        return sums

    def up(i):
        return lax.rem(my_group + i, groups)

    def down(i):
        return lax.rem(my_group + groups - i, groups)

    sums = state(up(1))
    pl.semaphore_wait(barrier, chips)
    share(0, up(1), u_send, u_pair, sums)

    @pl.loop(2, groups + 1)
    def _(i):
        share(0, up(i), u_send, u_pair, state(up(i)))
        total(0, 0, up(i - 1), u_send, u_pair, u_tot, u_recv)

    total(0, 0, up(groups), u_send, u_pair, u_tot, u_recv)

    def local_part(g):
        cs = cols(g)
        lifted = [mm(q_ref[:, c], w, 1, 0) for c, w in zip(cs, weights(g))]
        feats = [features(x) for x in lifted]
        scores = [mm(f, fk_s[:, c], 1, 1) for c, f in zip(cs, feats)]
        scores = [jnp.where(causal, x, 0.0).astype(BF16) for x in scores]
        nums = [mm(x, v_ref[:, c], 1, 0) for c, x in zip(cs, scores)]
        for k, c in enumerate(cs):
            fq_s[:, c] = feats[k]
            a_s[g * GROUP + k] = scores[k]
            num_s[:, c] = nums[k]

    half = groups // 2
    load_q.wait()
    pl.loop(0, half)(local_part)
    scan(0, 1, u_recv, p_send, p_chip, lambda i: i)
    pl.loop(half, groups)(local_part)

    load_y.wait()
    hand_out(1, 1, down(0), p_chip, u_send, u_pair, p_fwd, p_full, core == 1)

    @pl.loop(0, groups)
    def _(i):
        @pl.when(i + 1 < groups)
        def _():
            hand_out(1, 1, down(i + 1), p_chip, u_send, u_pair, p_fwd, p_full, core == 1)

        g = down(i)
        cs = cols(g)
        receive(1, g, p_fwd, p_full)
        prefixes = heads_of(p_full, g)
        fqs = [fq_s[:, c] for c in cs]
        nums = [num_s[:, c] + mm(f, p, 1, 0) for c, f, p in zip(cs, fqs, prefixes)]
        recips = [lax.rsqrt(jnp.mean(x * x, axis=-1, keepdims=True) + 1e-06) for x in nums]
        ys = [y_ref[:, c].astype(F32) for c in cs]
        inners = [jnp.mean(y * x, axis=-1, keepdims=True) for y, x in zip(ys, nums)]
        grads = [(r * (y - x * (r * r * m))).astype(BF16) for r, y, x, m in zip(recips, ys, nums, inners)]
        sums = [mm(f, x, 0, 0) for f, x in zip(fqs, grads)]
        for c, x, r, gr in zip(cs, nums, recips, grads):
            att_ref[:, c] = (x * r).astype(BF16)
            g_s[:, c] = gr
        store(0, g).start()
        share(2, g, r_send, r_pair, sums)

        @pl.when(i > 0)
        def _():
            total(2, 2, down(i - 1), r_send, r_pair, r_tot, r_recv)

    total(2, 2, down(groups - 1), r_send, r_pair, r_tot, r_recv)

    def adjoint_part(g):
        cs = cols(g)
        grads = [g_s[:, c] for c in cs]
        ws = weights(g)
        prefixes = heads_of(p_full, g)
        backs = [mm(x, v_ref[:, c], 1, 1) for x, c in zip(grads, cs)]
        backs = [jnp.where(causal, x, 0.0).astype(BF16) for x in backs]
        gfqs = [mm(b, fk_s[:, c], 1, 0) + mm(x, p, 1, 1) for b, c, x, p in zip(backs, cs, grads, prefixes)]
        fqs = [fq_s[:, c] for c in cs]
        gas = [(x * slope_of(f)).astype(BF16) for x, f in zip(gfqs, fqs)]
        qgs = [mm(x, w, 1, 1).astype(BF16) for x, w in zip(gas, ws)]
        wts = [mm(q_ref[:, c], x, 0, 0) for c, x in zip(cs, gas)]
        gfks = [mm(b, f, 0, 0) for b, f in zip(backs, fqs)]
        vgls = [mm(a_s[g * GROUP + k], x, 0, 0) for k, x in enumerate(grads)]
        for k, c in enumerate(cs):
            qg_ref[:, c] = qgs[k]
            wt_s[g * GROUP + k] = wts[k]
            gfk_s[:, c] = gfks[k]
            vgl_s[:, c] = vgls[k]
        store(1, g).start()

    pl.loop(0, half)(adjoint_part)
    scan(2, 3, r_recv, s_send, s_chip, lambda i: chips - 1 - i)
    pl.loop(half, groups)(adjoint_part)

    hand_out(3, 3, down(0), s_chip, r_send, r_pair, s_fwd, s_full, first_core)

    @pl.loop(0, groups)
    def _(i):
        @pl.when(i + 1 < groups)
        def _():
            hand_out(3, 3, down(i + 1), s_chip, r_send, r_pair, s_fwd, s_full, first_core)

        g = down(i)
        cs = cols(g)
        receive(3, g, s_fwd, s_full)
        suffixes = heads_of(s_full, g)
        fks = [fk_s[:, c] for c in cs]
        gfks = [gfk_s[:, c] + mm(v_ref[:, c], s, 1, 1) for c, s in zip(cs, suffixes)]
        gbs = [(x * slope_of(f)).astype(BF16) for x, f in zip(gfks, fks)]
        wts = [wt_s[g * GROUP + k] + mm(k_ref[:, c], x, 0, 0) for k, (c, x) in enumerate(zip(cs, gbs))]
        for c, x in zip(cs, gbs):
            gb_s[:, c] = x
        share(4, g, f_send, f_pair, wts)

        @pl.when(i > 0)
        def _():
            total(4, 4, down(i - 1), f_send, f_pair, f_tot, f_recv)

    total(4, 4, down(groups - 1), f_send, f_pair, f_tot, f_recv)

    @pl.loop(0, groups)
    def _(g):
        cs = cols(g)
        suffixes = heads_of(s_full, g)
        vgs = [vgl_s[:, c] + mm(fk_s[:, c], s, 1, 0) for c, s in zip(cs, suffixes)]
        kgs = [mm(gb_s[:, c], w, 1, 1) for c, w in zip(cs, weights(g))]
        for c, a, b in zip(cs, vgs, kgs):
            vg_ref[:, c] = a.astype(BF16)
            kg_ref[:, c] = b.astype(BF16)
        store(2, g).start()
        store(3, g).start()

    def collect(c, acc):
        wait_chip(4, f_recv, c)
        return acc + f_recv[c].astype(F32)

    fg_ref[...] = lax.fori_loop(0, chips, collect, jnp.zeros((rows, dh), F32), unroll=chips <= 8) * scale

    @pl.loop(0, groups)
    def _(g):
        for which in range(4):
            store(which, g).wait()

    for phase, buf in enumerate((u_tot, p_send, r_tot, s_send, f_tot)):
        some = buf.at[pl.ds(0, chips - 1)]
        pltpu.make_async_remote_copy(
            src_ref=some, dst_ref=some, send_sem=chip_send_sems.at[phase], recv_sem=chip_recv_sems.at[phase, 0],
            device_id={"seq": 2 * chip + other}, device_id_type=MESH).wait_send()
        to_pair(phase, 0, buf, buf).wait_send()


def copy_out(*refs):
    ins, outs, held = refs[:5], refs[5:10], refs[10:15]
    in_sems, out_sems = refs[15:]

    def parts(sources, targets, sems):
        copies = []
        for i, (source, target) in enumerate(zip(sources, targets)):
            size = source.shape[0] // PIECES
            for p in range(PIECES):
                some = pl.ds(p * size, size)
                copies.append(pltpu.make_async_copy(source.at[some], target.at[some], sems.at[i, p]))
        return copies

    reads = parts(ins, held, in_sems)
    writes = parts(held, outs, out_sems)
    for read in reads:
        read.start()
    for read, write in zip(reads, writes):
        read.wait()
        write.start()
    for write in writes:
        write.wait()


def local(queries, keys, values, feature_map, out_grad):
    tokens, width = queries.shape
    heads, dh, _ = feature_map.shape
    n = lax.axis_size("seq")
    chips, groups = n // 2, heads // GROUP
    rows = heads * dh // n
    wide = jax.ShapeDtypeStruct((tokens, width), BF16)
    vmem = pl.BlockSpec(memory_space=pltpu.VMEM)
    hbm = pl.BlockSpec(memory_space=pltpu.HBM)
    shapes = (wide, wide, wide, wide, jax.ShapeDtypeStruct((rows, dh), F32))
    outs = pl.pallas_call(
        functools.partial(kernel, n, heads, dh, 1.0 / math.sqrt(tokens * n)),
        out_shape=shapes,
        in_specs=[hbm] * 5,
        out_specs=(hbm,) * 4 + (vmem,),
        scratch_shapes=[pltpu.VMEM((tokens, width), BF16)] * 3 + [pltpu.VMEM((heads, dh, dh), BF16)] + [
            pltpu.VMEM((tokens, width), BF16)] * 8 + [
            pltpu.VMEM((heads, tokens, tokens), BF16),
            pltpu.VMEM((tokens, width), F32),
            pltpu.VMEM((tokens, width), F32),
            pltpu.VMEM((tokens, width), F32),
            pltpu.VMEM((heads, dh, dh), F32),
            pltpu.VMEM((tokens, width), BF16),
        ] + [pltpu.VMEM((chips, 2, rows, dh), BF16)] * 5 + [pltpu.VMEM((chips, rows, dh), BF16)] * 15 + [
            pltpu.SemaphoreType.DMA((5,)),
            pltpu.SemaphoreType.DMA((5, groups)),
            pltpu.SemaphoreType.DMA((5,)),
            pltpu.SemaphoreType.DMA((5, chips)),
            pltpu.SemaphoreType.DMA((3, groups)),
            pltpu.SemaphoreType.DMA((2,)),
            pltpu.SemaphoreType.DMA((4, groups)),
        ],
        compiler_params=pltpu.CompilerParams(
            collective_id=0, has_side_effects=True, vmem_limit_bytes=56 << 20),
        name="linear_attention",
    )(queries, keys, values, feature_map, out_grad)
    outs = pl.pallas_call(
        copy_out,
        out_shape=shapes,
        in_specs=[hbm] * 5,
        out_specs=(hbm,) * 5,
        scratch_shapes=[pltpu.VMEM(x.shape, x.dtype) for x in shapes] + [pltpu.SemaphoreType.DMA((5, PIECES))] * 2,
        compiler_params=pltpu.CompilerParams(vmem_limit_bytes=56 << 20),
        name="copy_out",
    )(*outs)
    return tuple(outs[:4]) + (outs[4].reshape(rows * dh),)


def solution(mesh):
    wide = P(("grp", "seq"), None)
    return jax.shard_map(
        local, mesh=mesh, in_specs=(wide, wide, wide, P(), wide),
        out_specs=(wide, wide, wide, wide, P(("grp", "seq"))), check_vma=False)
```
